32 devices in a mesh: seq: 32 (over z, y, x, core).
Axes of the slice: x: 2, y: 2, z: 4, core: 2. Of those that a mesh axis runs over, the one named last changes fastest.
Arguments:
- queries: bfloat16 [5120, 1024], P('seq'), may hold values from -8 to 8
- key_rows: bfloat16 [5120, 1024], P('seq'), may hold values from -8 to 8
- value_rows: bfloat16 [5120, 1024], P('seq'), may hold values from -6 to 6
- out_weight: bfloat16 [1048576], P('seq'), may hold values from -0.75 to 0.75
- cotangent: bfloat16 [5120, 1024], P('seq'), may hold values from -6 to 6
- row_lengths: int32 [25], replicated, may hold values from 1 to 400, 5120 in all
- window_shift: int32 [5120], P('seq'), may hold values from 0 to 720
Outputs:
- layer_out: bfloat16 [5120, 1024], P('seq')
- grad_queries: bfloat16 [5120, 1024], P('seq')
- grad_keys: bfloat16 [5120, 1024], P('seq')
- grad_values: bfloat16 [5120, 1024], P('seq')
- grad_weight: float32 [1048576], P('seq')
The draws below stay inside these ranges and needn't reach their ends.
All inputs are finite; a program needn't handle non-finite values.
Results may differ from the reference program's by a relative error of at most 0.025.
Values may be sent and summed in bfloat16 or wider, within the bound.
No kernel may reach another device: no remote copies, remote signals or barrier semaphores. Data moves between devices by JAX's collectives and lax.ppermute only.
A program may use at most 128 MiB of HBM per device.

```python
import math
import jax
import jax.numpy as jnp
import numpy as np
from jax import lax

D = 1024
HEADS = 16
HEAD = 64
WIN = 1120
MOSTROW = 400
PTS_DEV = 160
NPTS = 5120
ROWS = 25
HALO_DEV = 7


def draw_queries(key, part):
    noise_key = jax.random.fold_in(key, 17)
    result = jnp.clip(2.0 * jax.random.normal(noise_key, (NPTS, D), jnp.float32), -8.0, 8.0)
    return result.astype(jnp.bfloat16)


def draw_key_rows(key, part):
    noise_key = jax.random.fold_in(key, 29)
    result = jnp.clip(jax.random.normal(noise_key, (NPTS, D), jnp.float32), -8.0, 8.0)
    return result.astype(jnp.bfloat16)


def set_ends(array, key, least, high):
    longest = array.shape.index(max(array.shape))
    spots = []
    for shift in (0, 1):
        where = [jax.random.randint(jax.random.fold_in(key, axis), (), 0, length) for axis, length in enumerate(array.shape)]
        where[longest] = (where[longest] + shift) % array.shape[longest]
        spots.append(tuple(where))
    return array.at[spots[0]].set(least).at[spots[1]].set(high)


def levels(rng, shape, pieces, low, high):
    def one(dim, shards_of):
        draws = jax.random.uniform(jax.random.fold_in(jax.random.fold_in(rng, 6), dim), (shards_of,), jnp.float32, low / len(pieces), high / len(pieces))
        return jnp.repeat(jnp.exp(draws), shape[dim] // shards_of).reshape((-1,) + (1,) * (len(shape) - dim - 1))

    level = one(*pieces[0])
    for cut in pieces[1:]:
        level = level * one(*cut)
    return level


def profile(amount, total, limit, lean):
    weights = [(1 << 20) // math.isqrt(rank ** lean) + 1 for rank in range(2, amount + 1)]
    rest, given = total - limit - (amount - 1), [1] * (amount - 1)
    while rest > 0:
        movable = [i for i in range(amount - 1) if given[i] < limit]
        pool, left = sum([weights[i] for i in movable]), rest
        for i in movable:
            more = min(limit - given[i], max(1, left * weights[i] // pool), rest)
            given[i] = given[i] + more
            rest = rest - more
    return np.array([limit] + given)


def ragged(key, number_of, total, limit, slope):
    if number_of == 2:
        one = jax.random.randint(key, (), max(1, total - limit), min(limit, total - 1) + 1)
        return jnp.stack([one, total - one])
    tallies = jnp.asarray(profile(number_of, total, limit, slope), jnp.int32)
    twos = (number_of - 1) // 2
    donor, receiver = tallies[1:1 + 2 * twos:2], tallies[2:2 + 2 * twos:2]
    room = jnp.minimum(donor - 1, limit - receiver)
    moved = jax.random.randint(jax.random.fold_in(key, 1), (twos,), 0, 1 << 20) % (room + 1)
    tallies = tallies.at[1:1 + 2 * twos:2].set(donor - moved).at[2:2 + 2 * twos:2].set(receiver + moved)
    return tallies[jax.random.permutation(jax.random.fold_in(key, 2), number_of)]


def normal_values(stream_key, dims, width, reach, cuts=(), kind=jnp.bfloat16):
    drawn = width * jax.random.normal(stream_key, dims, jnp.float32)
    if cuts:
        drawn = drawn * levels(stream_key, dims, cuts, -0.22, 0.18)
    return jnp.clip(drawn, -reach, reach).astype(kind)


def setup_inputs(seed: int = 0) -> dict:
    key_list = jax.random.split(jax.random.key(seed), 8)
    queries = draw_queries(jax.random.fold_in(key_list[7], 71), 0)
    key_rows = draw_key_rows(jax.random.fold_in(key_list[7], 71), 0)
    value_rows = normal_values(key_list[2], (NPTS, D), 1.0, 6.0, ((0, 32),))
    out_weight = normal_values(key_list[3], (D * D,), (4.0 / D ** 0.5), 0.75, ((0, 32),))
    cotangent = normal_values(key_list[4], (NPTS, D), 1.0, 6.0, ((0, 32),))
    row_lengths = ragged(key_list[5], ROWS, NPTS, MOSTROW, 1).astype(jnp.int32)
    window_shift = set_ends(jax.random.randint(key_list[6], (NPTS,), 0, WIN - MOSTROW + 1), jax.random.fold_in(key_list[6], 1), 0, WIN - MOSTROW).astype(jnp.int32)
    return dict(queries=queries, key_rows=key_rows, value_rows=value_rows, out_weight=out_weight, cotangent=cotangent, row_lengths=row_lengths, window_shift=window_shift)


def head_view(block):
    return block.reshape(block.shape[0], HEADS, HEAD).astype(jnp.float32)


def window_starts(row_lengths, window_shift, first_point, all_points):
    point_index = first_point + jnp.arange(window_shift.shape[0], dtype=jnp.int32)
    row_ends = jnp.cumsum(row_lengths).astype(jnp.int32)
    passed = row_ends[None, :] <= point_index[:, None]
    row_first = jnp.sum(jnp.where(passed, row_lengths[None, :], 0), axis=1).astype(jnp.int32)
    return jnp.clip(row_first - window_shift, 0, all_points - WIN).astype(jnp.int32)


def reference(queries, key_rows, value_rows, out_weight, cotangent, row_lengths, window_shift):
    head_scale = 1.0 / (HEAD ** 0.5)
    margin = PTS_DEV * HALO_DEV
    rim_rows = (2 * HALO_DEV + 1) * PTS_DEV
    starts = window_starts(row_lengths, window_shift, 0, NPTS)
    keys_padded = jnp.pad(key_rows, ((margin, margin), (0, 0)))
    values_padded = jnp.pad(value_rows, ((margin, margin), (0, 0)))
    block_list = jnp.arange(NPTS // PTS_DEV, dtype=jnp.int32)

    def block_scores(block_index):
        first_point = (block_index * PTS_DEV).astype(jnp.int32)
        query_block = lax.dynamic_slice_in_dim(queries, first_point, PTS_DEV, 0)
        key_block = lax.dynamic_slice_in_dim(keys_padded, first_point, rim_rows, 0)
        start_block = lax.dynamic_slice_in_dim(starts, first_point, PTS_DEV, 0)
        key_index = first_point - margin + jnp.arange(rim_rows, dtype=jnp.int32)
        allowed = (key_index[None, :] >= start_block[:, None]) & (key_index[None, :] < start_block[:, None] + WIN)
        scores = jnp.einsum("qhd,khd->hqk", head_view(query_block), head_view(key_block)) * head_scale
        return jnp.where(allowed[None], scores, -jnp.inf)

    def forward_block(block_index):
        first_point = (block_index * PTS_DEV).astype(jnp.int32)
        scores = block_scores(block_index)
        value_block = head_view(lax.dynamic_slice_in_dim(values_padded, first_point, rim_rows, 0))
        row_top = jnp.max(scores, axis=2, keepdims=True)
        log_total = row_top + jnp.log(jnp.sum(jnp.exp(scores - row_top), axis=2, keepdims=True))
        softmax_out = lax.optimization_barrier(jnp.exp(scores - log_total).astype(jnp.bfloat16))
        mixed = jnp.einsum("hqk,khd->qhd", softmax_out.astype(jnp.float32), value_block)
        return mixed.reshape(PTS_DEV, D).astype(jnp.bfloat16), log_total[:, :, 0].T

    mixed, log_total = lax.map(forward_block, block_list)
    mixed = mixed.reshape(NPTS, D)
    log_total = log_total.reshape(NPTS, HEADS)
    square = out_weight.reshape(D, D)
    layer_out = jnp.dot(mixed, square, preferred_element_type=jnp.float32).astype(jnp.bfloat16)
    grad_mixed = jnp.dot(cotangent, square.T, preferred_element_type=jnp.float32).astype(jnp.bfloat16)
    grad_weight = (jnp.dot(mixed.T, cotangent, preferred_element_type=jnp.float32) * (1.0 / (NPTS ** 0.5))).reshape(D * D)
    row_delta = jnp.sum((grad_mixed.astype(jnp.float32) * mixed.astype(jnp.float32)).reshape(NPTS, HEADS, HEAD), axis=2)

    def backward_block(carry, block_index):
        keys_sum, values_sum = carry
        first_point = (block_index * PTS_DEV).astype(jnp.int32)
        scores = block_scores(block_index)
        query_block = head_view(lax.dynamic_slice_in_dim(queries, first_point, PTS_DEV, 0))
        key_block = head_view(lax.dynamic_slice_in_dim(keys_padded, first_point, rim_rows, 0))
        value_block = head_view(lax.dynamic_slice_in_dim(values_padded, first_point, rim_rows, 0))
        grad_block = head_view(lax.dynamic_slice_in_dim(grad_mixed, first_point, PTS_DEV, 0))
        total_block = lax.dynamic_slice_in_dim(log_total, first_point, PTS_DEV, 0).T[:, :, None]
        delta_block = lax.dynamic_slice_in_dim(row_delta, first_point, PTS_DEV, 0).T[:, :, None]
        chances = jnp.exp(scores - total_block)
        grad_scores = jnp.einsum("qhd,khd->hqk", grad_block, value_block)
        slopes = lax.optimization_barrier((chances * (grad_scores - delta_block)).astype(jnp.bfloat16)).astype(jnp.float32)
        rounded = lax.optimization_barrier(chances.astype(jnp.bfloat16)).astype(jnp.float32)
        grad_query = (jnp.einsum("hqk,khd->qhd", slopes, key_block) * head_scale).reshape(PTS_DEV, D).astype(jnp.bfloat16)
        key_part = jnp.einsum("hqk,qhd->khd", slopes, query_block).reshape(rim_rows, D)
        value_part = jnp.einsum("hqk,qhd->khd", rounded, grad_block).reshape(rim_rows, D)
        keys_sum = lax.dynamic_update_slice_in_dim(keys_sum, lax.dynamic_slice_in_dim(keys_sum, first_point, rim_rows, 0) + key_part, first_point, 0)
        values_sum = lax.dynamic_update_slice_in_dim(values_sum, lax.dynamic_slice_in_dim(values_sum, first_point, rim_rows, 0) + value_part, first_point, 0)
        return (keys_sum, values_sum), grad_query

    zeros_pad = jnp.zeros((NPTS + 2 * margin, D), jnp.float32)
    (keys_sum, values_sum), grad_queries = lax.scan(backward_block, (zeros_pad, zeros_pad), block_list)
    grad_queries = grad_queries.reshape(NPTS, D)
    grad_keys = (keys_sum[margin:margin + NPTS] * head_scale).astype(jnp.bfloat16)
    grad_values = values_sum[margin:margin + NPTS].astype(jnp.bfloat16)
    return layer_out, grad_queries, grad_keys, grad_values, grad_weight
```

```python
import functools
import math

import jax
import jax.numpy as jnp
from jax import lax
from jax.experimental import pallas as pl
from jax.experimental.pallas import tpu as pltpu
from jax.sharding import PartitionSpec as P

HEAD = 64
WIN = 1120
PAIR = 2 * HEAD
QBLOCK = 256
CHUNK = 256
LANES = 128
SUB = 16
DIGIT = 32
VMEM_LIMIT = 60 * 1024 * 1024


def up(value, step):
    return (value + step - 1) // step * step


def whole(shape):
    return pl.BlockSpec(shape, lambda *_: (0,) * len(shape))


def nt_dot(a, b):
    return lax.dot_general(a, b, (((1,), (1,)), ((), ())), preferred_element_type=jnp.float32)


def nn_dot(a, b):
    return lax.dot_general(a, b, (((1,), (0,)), ((), ())), preferred_element_type=jnp.float32)


def call(kernel, out_shape, flops=0, moved=0, exps=0, **kwargs):
    return pl.pallas_call(
        kernel,
        out_shape=out_shape,
        compiler_params=pltpu.CompilerParams(vmem_limit_bytes=VMEM_LIMIT),
        cost_estimate=pl.CostEstimate(flops=flops, bytes_accessed=moved, transcendentals=exps),
        **kwargs,
    )


def pack_kernel(points, q_ref, k_ref, v_ref, extra_ref, x_ref):
    for peer in range(x_ref.shape[0]):
        cols = slice(peer * PAIR, (peer + 1) * PAIR)
        x_ref[peer, 0:points, :] = q_ref[:, cols]
        x_ref[peer, points:2 * points, :] = k_ref[:, cols]
        x_ref[peer, 2 * points:3 * points, :] = v_ref[:, cols]
        x_ref[peer, 3 * points:, :] = extra_ref[...]


def block_range(start_row):
    low = jnp.min(start_row) // LANES * LANES
    high = jnp.max(start_row) + WIN
    return pl.multiple_of(low, LANES), (high - low + CHUNK - 1) // CHUNK


def head_rows(block, head):
    lane = lax.broadcasted_iota(jnp.int32, block.shape, 1)
    keep = (lane >= head * HEAD) & (lane < (head + 1) * HEAD)
    return jnp.where(keep, block, jnp.zeros_like(block))


def forward_kernel(
    points, reach, offset,
    x_ref, low_ref, high_ref, start_ref,
    p_ref, mixt_ref, mix_ref, inv_ref, q_ref, k_ref, v_ref, kt_ref,
    s_ref, vt_ref, acc_ref,
):
    group = x_ref.shape[0]
    total = k_ref.shape[0]

    @pl.when(pl.program_id(0) == 0)
    def _():
        for ref, base in ((k_ref, 0), (v_ref, points)):
            row = offset - reach * points
            if row:
                ref[0:row, :] = jnp.zeros((row, PAIR), ref.dtype)
            for j in range(reach):
                ref[row:row + points, :] = low_ref[j, base:base + points, :]
                row += points
            for j in range(group):
                ref[row:row + points, :] = x_ref[j, points + base:2 * points + base, :]
                row += points
            for j in range(reach):
                ref[row:row + points, :] = high_ref[j, base:base + points, :]
                row += points
            ref[row:, :] = jnp.zeros((total - row, PAIR), ref.dtype)
        for j in range(group):
            q_ref[j * points:(j + 1) * points, :] = x_ref[j, 0:points, :] * (1.0 / math.sqrt(HEAD))
        for t in range(total // LANES):
            rows = slice(t * LANES, (t + 1) * LANES)
            kt_ref[:, rows] = k_ref[rows, :].T
            vt_ref[:, rows] = v_ref[rows, :].T

    block = pl.program_id(0)
    start_row = start_ref[...]
    low, chunks = block_range(start_row)
    q_block = q_ref[pl.ds(pl.multiple_of(block * QBLOCK, QBLOCK), QBLOCK), :]
    q_heads = [head_rows(q_block, h) for h in range(2)]
    key_row = lax.broadcasted_iota(jnp.int32, (CHUNK, QBLOCK), 0) - start_row

    def score_chunk(c, tops):
        base = pl.multiple_of(low + c * CHUNK, LANES)
        keys = k_ref[pl.ds(base, CHUNK), :]
        spot = key_row + base
        valid = (spot >= 0) & (spot < WIN)
        result = []
        for h in range(2):
            scores = jnp.where(valid, nt_dot(keys, q_heads[h]), -jnp.inf)
            s_ref[h, pl.ds(pl.multiple_of(c * CHUNK, CHUNK), CHUNK), :] = scores
            result.append(jnp.maximum(tops[h], jnp.max(scores.reshape(CHUNK // 8, 8, QBLOCK), axis=0)))
        return tuple(result)

    empty = jnp.full((8, QBLOCK), -jnp.inf, jnp.float32)
    tops = lax.fori_loop(0, chunks, score_chunk, (empty, empty))
    tops = [jnp.max(top, axis=0, keepdims=True) for top in tops]
    acc_ref[...] = jnp.zeros_like(acc_ref)

    def mix_chunk(c, sums):
        base = pl.multiple_of(low + c * CHUNK, LANES)
        rows = pl.ds(pl.multiple_of(c * CHUNK, CHUNK), CHUNK)
        result = []
        for h in range(2):
            weights = jnp.exp(s_ref[h, rows, :] - tops[h])
            rounded = weights.astype(jnp.bfloat16)
            p_ref[0, h, rows, :] = rounded
            acc_ref[h] += nn_dot(vt_ref[h * HEAD:(h + 1) * HEAD, pl.ds(base, CHUNK)], rounded)
            result.append(sums[h] + jnp.sum(weights.reshape(CHUNK // 8, 8, QBLOCK), axis=0))
        return tuple(result)

    none = jnp.zeros((8, QBLOCK), jnp.float32)
    sums = lax.fori_loop(0, chunks, mix_chunk, (none, none))
    inverse = [1.0 / jnp.sum(part, axis=0, keepdims=True) for part in sums]
    mixed = jnp.concatenate([acc_ref[h] * inverse[h] for h in range(2)], axis=0)
    mixt_ref[...] = mixed.astype(jnp.bfloat16)
    mix_ref[...] = mixed.T.astype(jnp.bfloat16)
    inv_ref[...] = jnp.concatenate([jnp.broadcast_to(part, (4, QBLOCK)) for part in inverse], axis=0)


def backward_kernel(
    points, reach, offset, scale,
    place_ref, start_ref, p_ref, mixt_ref, inv_ref, q_ref, k_ref, v_ref, kt_ref, w_ref, *rest,
):
    group = (q_ref.shape[0]) // points
    cot_refs = rest[:group]
    dq_ref, low_ref, high_ref, own_ref, gw_ref, cot_ref, dk_ref, dv_ref, acc_ref = rest[group:]
    block = pl.program_id(0)
    rows = pl.ds(pl.multiple_of(block * QBLOCK, QBLOCK), QBLOCK)

    @pl.when(block == 0)
    def _():
        place = place_ref[0]
        for j in range(group):
            spot = pl.multiple_of((place ^ j) * points, SUB)
            cot_ref[pl.ds(spot, points), :] = cot_refs[j][...]
        dk_ref[...] = jnp.zeros_like(dk_ref)
        dv_ref[...] = jnp.zeros_like(dv_ref)
        gw_ref[...] = jnp.zeros_like(gw_ref)

    low, chunks = block_range(start_ref[...])
    cot_block = cot_ref[rows, :]
    gw_ref[...] += nn_dot(mixt_ref[...], cot_block) * scale
    grad = nt_dot(w_ref[...], cot_block).astype(jnp.bfloat16).astype(jnp.float32)
    q_block = q_ref[rows, :]
    row_id = lax.broadcasted_iota(jnp.int32, (PAIR, QBLOCK), 0)
    grads_t, grads, deltas, q_heads = [], [], [], []
    for h in range(2):
        keep = (row_id >= h * HEAD) & (row_id < (h + 1) * HEAD)
        part = jnp.where(keep, grad * inv_ref[4 * h:4 * h + 1, :], 0.0)
        rounded = part.astype(jnp.bfloat16)
        part = rounded.astype(jnp.float32)
        deltas.append(jnp.sum(part * mixt_ref[...].astype(jnp.float32), axis=0, keepdims=True))
        grads_t.append(rounded)
        grads.append(part.T.astype(jnp.bfloat16))
        q_heads.append(head_rows(q_block, h))
    acc_ref[...] = jnp.zeros_like(acc_ref)

    def chunk_step(c, carry):
        base = pl.multiple_of(low + c * CHUNK, LANES)
        spot = pl.ds(base, CHUNK)
        part = pl.ds(pl.multiple_of(c * CHUNK, CHUNK), CHUNK)
        values = v_ref[spot, :]
        dk, dv = dk_ref[spot, :], dv_ref[spot, :]
        for h in range(2):
            chance = p_ref[0, h, part, :]
            slope = nn_dot(values, grads_t[h]) - deltas[h]
            slope = (chance.astype(jnp.float32) * slope).astype(jnp.bfloat16)
            acc_ref[h] += nn_dot(kt_ref[h * HEAD:(h + 1) * HEAD, spot], slope)
            dk += nn_dot(slope, q_heads[h])
            dv += nn_dot(chance, grads[h])
        dk_ref[spot, :] = dk
        dv_ref[spot, :] = dv
        return carry

    lax.fori_loop(0, chunks, chunk_step, 0)
    grad_q = jnp.concatenate([acc_ref[h] for h in range(2)], axis=0) * (1.0 / math.sqrt(HEAD))
    dq_ref[...] = grad_q.T.astype(jnp.bfloat16)

    @pl.when(block == pl.num_programs(0) - 1)
    def _():
        for ref, base in ((dk_ref, 0), (dv_ref, points)):
            row = offset - reach * points
            for j in range(reach):
                low_ref[j, base:base + points, :] = ref[row:row + points, :].astype(jnp.bfloat16)
                row += points
            for j in range(group):
                own_ref[j, base:base + points, :] = ref[row:row + points, :]
                row += points
            for j in range(reach):
                high_ref[j, base:base + points, :] = ref[row:row + points, :].astype(jnp.bfloat16)
                row += points


def add_kernel(own_ref, below_ref, above_ref, out_ref):
    group, reach = own_ref.shape[0], below_ref.shape[0]
    for j in range(group):
        value = own_ref[j]
        if j < reach:
            value += below_ref[j].astype(jnp.float32)
        if j >= group - reach:
            value += above_ref[j - (group - reach)].astype(jnp.float32)
        out_ref[j] = value.astype(jnp.bfloat16)


def layer_kernel(points, place_ref, y_ref, *rest):
    group = y_ref.shape[0]
    w_refs = rest[:group]
    layer_ref, dq_ref = rest[group:]
    place = place_ref[0]
    total = nn_dot(y_ref[place, 0:points, :], w_refs[0][...])
    for j in range(1, group):
        total += nn_dot(y_ref[place ^ j, 0:points, :], w_refs[j][...])
    layer_ref[...] = total.astype(jnp.bfloat16)
    for j in range(group):
        dq_ref[:, j * PAIR:(j + 1) * PAIR] = y_ref[j, points:, :]


def split_kernel(points, y_ref, dk_ref, dv_ref):
    for j in range(y_ref.shape[0]):
        cols = slice(j * PAIR, (j + 1) * PAIR)
        dk_ref[:, cols] = y_ref[j, 0:points, :]
        dv_ref[:, cols] = y_ref[j, points:, :]


def permute(block, move):
    devices = range(lax.axis_size("seq"))
    return lax.ppermute(block, "seq", [(i, move(i)) for i in devices if move(i) in devices])


def gather_group(block, group):
    pieces = {0: block}
    for j in range(2, group, 2):
        pieces[j] = permute(block, lambda i, j=j: i ^ j)
    for j in range(0, group, 2):
        pieces[j + 1] = permute(pieces[j], lambda i: i ^ 1)
    return [pieces[j] for j in range(group)]


def per_device(queries, key_rows, value_rows, out_weight, cotangent, row_lengths, window_shift):
    points, width = queries.shape
    devices = lax.axis_size("seq")
    group = width // PAIR
    planes = devices // group
    all_points = points * devices
    plane_points = points * group
    reach = (WIN - 2 + points) // points
    offset = up(reach * points, LANES)
    span = 2 * offset + QBLOCK
    blocks = plane_points // QBLOCK
    total = up((blocks - 1) * QBLOCK + span + LANES, LANES)
    device = lax.axis_index("seq")
    plane, place = device // group, device % group
    place_list = place.reshape(1)
    groups = [[g * group + p for p in range(group)] for g in range(planes)]
    bf16, f32 = jnp.bfloat16, jnp.float32

    def shape(dims, kind=bf16):
        return jax.ShapeDtypeStruct(dims, kind)

    extra_rows = up(-(-2 * points // PAIR), SUB)
    digits = jnp.concatenate([window_shift // DIGIT, window_shift % DIGIT]).astype(bf16)
    extra = jnp.pad(digits, (0, extra_rows * PAIR - 2 * points)).reshape(extra_rows, PAIR)
    rows = 3 * points + extra_rows
    packed = call(
        functools.partial(pack_kernel, points), shape((group, rows, PAIR)),
        moved=12 * points * width,
    )(queries, key_rows, value_rows, extra)

    weight = out_weight.reshape(-1, width)
    part_rows = weight.shape[0]
    got = []
    for s in range(planes):
        got.append(permute(weight, lambda i, s=s: (i % planes + s) % planes * group + i // planes))
    order = jnp.stack(got[::-1] + got[::-1])
    own_weight = lax.dynamic_slice_in_dim(order, planes - 1 - plane, planes, 0).reshape(planes * part_rows, width)
    cots = gather_group(cotangent, group)

    swapped = lax.all_to_all(packed, "seq", 0, 0, tiled=True, axis_index_groups=groups)
    low_halo = permute(swapped[group - reach:, points:3 * points], lambda i: i + group)
    high_halo = permute(swapped[:reach, points:3 * points], lambda i: i - group)

    point_index = plane * plane_points + jnp.arange(plane_points, dtype=jnp.int32)
    passed = jnp.cumsum(row_lengths)[None, :] <= point_index[:, None]
    row_first = jnp.sum(jnp.where(passed, row_lengths[None, :], 0), axis=1)
    codes = swapped[:, 3 * points:].reshape(group, extra_rows * PAIR).astype(jnp.int32)
    shifts = (codes[:, :points] * DIGIT + codes[:, points:2 * points]).reshape(plane_points)
    starts = jnp.clip(row_first - shifts, 0, all_points - WIN) - plane * plane_points + offset
    starts = starts.reshape(1, plane_points)

    start_spec = pl.BlockSpec((1, QBLOCK), lambda b, *_: (0, b))
    chance_spec = pl.BlockSpec((1, 2, span, QBLOCK), lambda b, *_: (b, 0, 0, 0))
    column_spec = pl.BlockSpec((PAIR, QBLOCK), lambda b, *_: (0, b))
    row_spec = pl.BlockSpec((QBLOCK, PAIR), lambda b, *_: (b, 0))
    inverse_spec = pl.BlockSpec((8, QBLOCK), lambda b, *_: (0, b))
    work = 2 * 2 * plane_points * span * HEAD
    chances, mixed_t, mixed, inverse, q_all, k_all, v_all, kt_all = call(
        functools.partial(forward_kernel, points, reach, offset),
        (
            shape((blocks, 2, span, QBLOCK)), shape((PAIR, plane_points)), shape((plane_points, PAIR)),
            shape((8, plane_points), f32), shape((plane_points, PAIR)), shape((total, PAIR)),
            shape((total, PAIR)), shape((PAIR, total)),
        ),
        flops=8 * work, moved=40 * plane_points * PAIR, exps=2 * plane_points * span,
        grid=(blocks,),
        in_specs=[whole(swapped.shape), whole(low_halo.shape), whole(high_halo.shape), start_spec],
        out_specs=(
            chance_spec, column_spec, row_spec, inverse_spec, whole((plane_points, PAIR)),
            whole((total, PAIR)), whole((total, PAIR)), whole((PAIR, total)),
        ),
        scratch_shapes=[
            pltpu.VMEM((2, span, QBLOCK), f32), pltpu.VMEM((PAIR, total), bf16),
            pltpu.VMEM((2, HEAD, QBLOCK), f32),
        ],
    )(swapped, low_halo, high_halo, starts)

    weights = gather_group(own_weight, group)
    grad_q, low_part, high_part, own_part, weight_part = call(
        functools.partial(backward_kernel, points, reach, offset, 1.0 / math.sqrt(all_points)),
        (
            shape((plane_points, PAIR)), shape((reach, 2 * points, PAIR)), shape((reach, 2 * points, PAIR)),
            shape((group, 2 * points, PAIR), f32), shape((PAIR, width), f32),
        ),
        flops=16 * work, moved=40 * plane_points * PAIR,
        grid_spec=pltpu.PrefetchScalarGridSpec(
            num_scalar_prefetch=1,
            grid=(blocks,),
            in_specs=[
                start_spec, chance_spec, column_spec, inverse_spec, whole((plane_points, PAIR)),
                whole((total, PAIR)), whole((total, PAIR)), whole((PAIR, total)), whole((PAIR, width)),
            ] + [whole((points, width))] * group,
            out_specs=(
                row_spec, whole((reach, 2 * points, PAIR)), whole((reach, 2 * points, PAIR)),
                whole((group, 2 * points, PAIR)), whole((PAIR, width)),
            ),
            scratch_shapes=[
                pltpu.VMEM((plane_points, width), bf16), pltpu.VMEM((total, PAIR), f32),
                pltpu.VMEM((total, PAIR), f32), pltpu.VMEM((2, HEAD, QBLOCK), f32),
            ],
        ),
    )(place_list, starts, chances, mixed_t, inverse, q_all, k_all, v_all, kt_all, own_weight, *cots)

    from_above = permute(low_part, lambda i: i - group)
    from_below = permute(high_part, lambda i: i + group)
    shares = []
    for s in range(planes):
        piece = lax.dynamic_slice_in_dim(weight_part, (plane + s) % planes * part_rows, part_rows, 0)
        shares.append(permute(piece, lambda i, s=s: i % group * planes + (i // group + s) % planes))
    first = jnp.concatenate(
        [mixed.reshape(group, points, PAIR), grad_q.reshape(group, points, PAIR)], axis=1
    )
    first = lax.all_to_all(first, "seq", 0, 0, tiled=True, axis_index_groups=groups)
    layer_out, grad_queries = call(
        functools.partial(layer_kernel, points), (shape((points, width)), shape((points, width))),
        flops=2 * points * width * width, moved=2 * width * width + 8 * points * width,
        grid_spec=pltpu.PrefetchScalarGridSpec(
            num_scalar_prefetch=1,
            grid=(1,),
            in_specs=[whole(first.shape)] + [whole((PAIR, width))] * group,
            out_specs=(whole((points, width)), whole((points, width))),
        ),
    )(place_list, first, *weights)
    summed = call(
        add_kernel, shape((group, 2 * points, PAIR)), moved=16 * points * width,
    )(own_part, from_below, from_above)
    summed = lax.all_to_all(summed, "seq", 0, 0, tiled=True, axis_index_groups=groups)
    grad_keys, grad_values = call(
        functools.partial(split_kernel, points), (shape((points, width)), shape((points, width))),
        moved=8 * points * width,
    )(summed)
    grad_weight = sum(shares[1:], shares[0]).reshape(part_rows * width)
    return (layer_out, grad_queries, grad_keys, grad_values, grad_weight)


def solution(mesh):
    rows = P("seq", None)
    return jax.shard_map(
        per_device,
        mesh=mesh,
        in_specs=(rows, rows, rows, P("seq"), rows, P(), P("seq")),
        out_specs=(rows, rows, rows, rows, P("seq")),
        check_vma=False,
    )
```
